32 devices in a mesh: groups: 2 (over y), gz: 4 (over z), view: 2 (over x), gy: 2 (over core).
Axes of the slice: x: 2, y: 2, z: 4, core: 2. Of those that a mesh axis runs over, the one named last changes fastest.
Arguments:
- camera: float32 [2, 256, 3, 128, 128], P('view', ('groups', 'gz'), None, 'gy'), parts along dimension 1, may hold values from 0 to 4
- background: int32 [2, 2, 8], P('view', 'gy', ('groups', 'gz')), parts along dimension 2, may hold values from 0 to 2
- destination: int32 [2, 2, 256, 1], P('view', 'gy', ('groups', 'gz')), parts along dimension 2, may hold values from 0 to 3; in each aligned block of 32 rows (0 to 31, 32 to 63, ..., all dimensions but the last counted through in order) at most 16 rows name the same one
- offsets: int32 [2, 2, 256], P('view', 'gy', ('groups', 'gz')), parts along dimension 2, may hold values from 0 to 6
- shift_frac: float32 [2, 3], P('view'), may hold values from 0.15 to 0.85
- psf_taps: float32 [2, 3, 9], P('view'), may hold values from 0.05 to 1
Outputs:
- estimate: float32 [64, 128, 128], P(('groups', 'gz'), 'gy'), parts along dimension 0
- joined_views: float32 [2, 64, 128, 128], P('view', ('groups', 'gz'), 'gy'), parts along dimension 1
The draws below stay inside these ranges and needn't reach their ends.
There are 2 independent parts, one for each index of `groups`. The reference program is written for one: setup_inputs(seed, part) draws one part's arguments, and reference() takes and returns one part's arrays. A program takes and returns all parts, laid end to end along the dimension named above; an argument that names none is the same for every part. Nothing has to cross between parts.
Inputs may be any that keep to these rules, and one draw needn't show every extreme that they name: `destination`: within the 32 block rows of one tile, no slab is named more than 16 times; some tile names one slab exactly 16 times.
All inputs are finite; a program needn't handle non-finite values.
Results may differ from the reference program's by a relative error of at most 0.0001.
Values sent between devices are 32-bit elements; how exact they have to be, the bound alone decides.
A program may use at most 64 MiB of HBM per device.

```python
import math
import jax
import jax.numpy as jnp
import numpy as np
from jax import lax

CZ = 8
CY = 64
CX = 128
NB = 32
BZ = 3
TAPS = 9
ITERS = 2
VIEWS = 2
MOST = 16
NZ = 32
NY = 128
NBLK = 128
N_GZ = 4
N_GY = 2


def touch_ends(values, own_key, low, largest):
    index_at = [jax.random.randint(jax.random.fold_in(own_key, axis), (), 0, length) for axis, length in enumerate(values.shape)]
    widest = values.shape.index(max(values.shape))
    beside = index_at[:widest] + [(index_at[widest] + 1) % values.shape[widest]] + index_at[widest + 1:]
    return values.at[tuple(index_at)].set(low).at[tuple(beside)].set(largest)


def block_scale(stream_key, extent, cuts, least, largest):
    factor_of = 1.0
    for axis_at, shards_of in cuts:
        steps = jax.random.uniform(jax.random.fold_in(jax.random.fold_in(stream_key, 6), axis_at), (shards_of,), jnp.float32, least / len(cuts), largest / len(cuts))
        factor_of = factor_of * jnp.repeat(jnp.exp(steps), extent[axis_at] // shards_of).reshape((-1,) + (1,) * (len(extent) - 1 - axis_at))
    return factor_of


def shared_out(rng, own, number, rows, count, top, bound, slope):
    ranking = jax.random.permutation(rng, count)
    crowded, usual = load_shares(count, rows * top, bound, slope, True), load_shares(count, rows * top, bound, slope, False)
    places = jnp.arange(count)

    def named(tallies, turn):
        used = int((tallies > 0).sum())
        fixed = max(1, used // 4)
        shifted = fixed + (places - fixed + turn * (used - fixed)) % max(1, count - fixed)
        return jnp.zeros((count,), jnp.int32).at[ranking[jnp.where(places < fixed, places, shifted)]].set(jnp.asarray(tallies, jnp.int32))

    tallies = jnp.where(number % 4 == 0, named(crowded, number // 4), named(usual, number - number // 4 - 1))
    mixed = jax.random.permutation(jax.random.fold_in(own, 3), count)
    giver, receiver = mixed[0:count // 2 * 2:2], mixed[1:count // 2 * 2:2]
    room = jnp.minimum(tallies[giver] - 1, bound - tallies[receiver]) // 2
    room = jnp.where((giver == ranking[0]) | (receiver == ranking[0]) | (tallies[receiver] == 0), 0, jnp.maximum(room, 0))
    shifted = jax.random.randint(jax.random.fold_in(own, 4), (count // 2,), 0, 1 << 20) % (room + 1)
    tallies = tallies.at[giver].add(-shifted).at[receiver].add(shifted)
    members = jnp.searchsorted(jnp.cumsum(tallies), jnp.arange(rows * top), side="right").astype(jnp.int32)
    listing = members.reshape(top, rows).T
    listing = listing[jax.random.permutation(jax.random.fold_in(own, 1), rows)]
    turn = jax.random.randint(jax.random.fold_in(own, 2), (rows, 1), 0, top)
    return jnp.take_along_axis(listing, (jnp.arange(top)[None, :] + turn) % top, axis=1)


def load_shares(amount, total, reach, lean, full):
    loads = [(1 << 20) // math.isqrt(rank ** lean) + 1 for rank in range(1, amount + 1)]
    largest = reach if full else min(reach, max(-(-total // amount), total * loads[0] // sum(loads)))
    least = 1 if total - largest >= amount - 1 else 0
    holding, spare = [largest] + [least] * (amount - 1), total - largest - least * (amount - 1)
    while spare > 0:
        free = [i for i in range(1, amount) if holding[i] < largest] or [i for i in range(1, amount) if holding[i] < reach]
        whole, budget = sum([loads[i] for i in free]), spare
        for i in free:
            extra = min(reach - holding[i], max(1, budget * loads[i] // whole), spare)
            holding[i] = holding[i] + extra
            spare = spare - extra
    return np.array(holding)


def setup_inputs(seed: int = 0, part: int = 0) -> dict:
    seeds = jax.random.split(jax.random.key(seed), 7)
    own_keys = jax.random.split(jax.random.fold_in(seeds[6], part), 7)
    camera = jnp.clip(4.0 * jax.random.uniform(own_keys[0], (VIEWS, NBLK, BZ, NY, CX), jnp.float32) ** block_scale(own_keys[0], (VIEWS, NBLK, BZ, NY, CX), ((0, 2), (1, 4), (3, 2)), -0.2, 0.2), 0.0, 4.0)
    background = touch_ends(jax.random.randint(own_keys[1], (VIEWS, N_GY, N_GZ), 0, 3), jax.random.fold_in(own_keys[1], 1), 0, 2).astype(jnp.int32)
    destination_keys = jax.random.split(jax.random.fold_in(own_keys[2], 1), VIEWS * N_GY * NBLK // NB)
    destination_turns = jax.random.permutation(jax.random.fold_in(own_keys[2], 3), VIEWS * N_GY * NBLK // NB)
    destination = jax.vmap(lambda own, number: shared_out(jax.random.fold_in(own_keys[2], 2), own, number, NB, N_GZ, 1, MOST, 2))(destination_keys, destination_turns).reshape((VIEWS, N_GY, NBLK, 1))
    offsets = touch_ends(jax.random.randint(own_keys[3], (VIEWS, N_GY, NBLK), 0, CZ - 1), jax.random.fold_in(own_keys[3], 1), 0, (CZ - 1) - 1).astype(jnp.int32)
    shift_frac = jnp.clip(0.15 + 0.70000002 * jax.random.uniform(seeds[4], (VIEWS, 3), jnp.float32) ** block_scale(seeds[4], (VIEWS, 3), ((0, 2),), -0.2, 0.2), 0.15, 0.85)
    psf_taps = jnp.clip(jnp.exp(math.log(1.0) - 2.9957323 * jax.random.uniform(seeds[5], (VIEWS, 3, TAPS), jnp.float32) ** block_scale(seeds[5], (VIEWS, 3, TAPS), ((0, 2),), -0.2, 0.2)), 0.05, 1.0)
    return {"camera": camera, "background": background, "destination": destination, "offsets": offsets, "shift_frac": shift_frac, "psf_taps": psf_taps}


DATA_FLOOR = 0.25
PRECISE = lax.Precision.HIGHEST


def interp_matrix(length, fraction):
    places = jnp.arange(length, dtype=jnp.int32)
    follow = jnp.minimum(places + 1, length - 1)
    same_row = (places[:, None] == places[None, :]).astype(jnp.float32)
    next_row = (follow[:, None] == places[None, :]).astype(jnp.float32)
    return (1.0 - fraction) * same_row + fraction * next_row


def interp_blocks(blocks, fraction_z, y_matrix, x_matrix):
    lower = blocks[..., :-1, :, :]
    upper = blocks[..., 1:, :, :]
    planes = (1.0 - fraction_z) * lower + fraction_z * upper
    planes = jnp.einsum("ry,...yx->...rx", y_matrix, planes, precision=PRECISE)
    return jnp.einsum("...rx,cx->...rc", planes, x_matrix, precision=PRECISE)


def along_last(volume, weights):
    margin = weights.shape[0] // 2
    span_cells = volume.shape[-1]
    padded = jnp.pad(volume, [(0, 0)] * (volume.ndim - 1) + [(margin, margin)])
    result = weights[0] * padded[..., 0:span_cells]
    for offset in range(1, weights.shape[0]):
        result = result + weights[offset] * padded[..., offset:offset + span_cells]
    return result


def valid_pass(padded, weights, out_len, along_axis):
    result = weights[0] * lax.slice_in_dim(padded, 0, out_len, axis=along_axis)
    for offset in range(1, weights.shape[0]):
        result = result + weights[offset] * lax.slice_in_dim(padded, offset, offset + out_len, axis=along_axis)
    return result


def apply_passes(padded, kernel, planes_out, rows_out):
    x_done = along_last(padded, kernel[2])
    y_done = valid_pass(x_done, kernel[1], rows_out, 1)
    return valid_pass(y_done, kernel[0], planes_out, 0)


def blur_whole(volume, kernel):
    margin = kernel.shape[1] // 2
    padded = jnp.pad(volume, ((margin, margin), (margin, margin), (0, 0)))
    return apply_passes(padded, kernel, volume.shape[0], volume.shape[1])


def reference(camera, background, destination, offsets, shift_frac, psf_taps):
    joined_list = []
    for view_idx in range(VIEWS):
        fraction = shift_frac[view_idx]
        y_matrix = interp_matrix(CY, fraction[1])
        x_matrix = interp_matrix(CX, fraction[2])
        columns = []
        for row_idx in range(N_GY):
            tiles = camera[view_idx, :, :, row_idx * CY:(row_idx + 1) * CY, :]
            levels = jnp.repeat(background[view_idx, row_idx], NB).astype(jnp.float32)
            blocks = tiles - levels[:, None, None, None]
            planes = interp_blocks(blocks, fraction[0], y_matrix, x_matrix)
            start_plane = destination[view_idx, row_idx, :, 0] * CZ + offsets[view_idx, row_idx]
            target = (start_plane[:, None] + jnp.arange(BZ - 1, dtype=jnp.int32)[None, :]).reshape(-1).astype(jnp.int32)
            total = jax.ops.segment_sum(planes.reshape(-1, CY, CX), target, num_segments=NZ)
            covered = jax.ops.segment_sum(jnp.ones(target.shape, jnp.float32), target, num_segments=NZ)
            columns.append(jnp.maximum(total / (covered[:, None, None] + 1.0), DATA_FLOOR))
        joined_list.append(jnp.concatenate(columns, axis=1))
    joined_views = jnp.stack(joined_list)
    kernels = psf_taps / jnp.sum(psf_taps, axis=-1, keepdims=True)
    estimate = jnp.sum(joined_views, axis=0) / VIEWS
    for iteration in range(ITERS):
        log_total = jnp.zeros(estimate.shape, jnp.float32)
        for view_idx in range(VIEWS):
            blurred = blur_whole(estimate, kernels[view_idx])
            ratio = joined_views[view_idx] / blurred
            correction = blur_whole(ratio, kernels[view_idx][:, ::-1])
            log_total = log_total + jnp.log(correction)
        estimate = estimate * jnp.exp(log_total / VIEWS)
    return estimate, joined_views
```

```python
import functools

import jax
import jax.numpy as jnp
from jax import lax
from jax.experimental import pallas as pl
from jax.experimental.pallas import tpu as pltpu
from jax.sharding import PartitionSpec as P

CZ = 8
ITERS = 2
HALO = 8
CHUNK = 4

DATA_FLOOR = 0.25
PRECISE = lax.Precision.HIGHEST
MESH = pl.DeviceIdType.MESH


def deposit_kernel(rows, dest, offs, level, frac, psf, cam_ref, acc_ref, tap_ref):
    step = pl.program_id(0)
    taps = psf.shape[1]

    @pl.when(step == 0)
    def _():
        @pl.loop(0, acc_ref.shape[0])
        def _(s):
            acc_ref[s] = jnp.zeros(acc_ref.shape[1:], jnp.float32)

        tap_ref[...] = jnp.zeros(tap_ref.shape, jnp.float32)
        for axis in range(3):
            scale = psf[axis, 0]
            for t in range(1, taps):
                scale = scale + psf[axis, t]
            scale = jnp.full((1, 128), scale, jnp.float32)
            for t in range(taps):
                at = axis * taps + t
                tap_ref[at : at + 1, :] = jnp.full((1, 128), psf[axis, t], jnp.float32) / scale

    fz = frac[0]
    base = level[0].astype(jnp.float32)
    for i in range(cam_ref.shape[0]):
        b = step * cam_ref.shape[0] + i
        s = dest[b]
        o = offs[b]
        lower = cam_ref[i, 0] - base
        for k in range(cam_ref.shape[1] - 1):
            upper = cam_ref[i, k + 1] - base
            at = pl.ds(pl.multiple_of((o + k) * rows, 8), rows)
            acc_ref[s, at, :] = acc_ref[s, at, :] + ((1.0 - fz) * lower + fz * upper)
            cnt = pl.ds(CZ * rows + o + k, 1)
            acc_ref[s, cnt, :] = acc_ref[s, cnt, :] + 1.0
            lower = upper


def world_kernel(
    dims, rows, taps,
    frac, acc_ref, tap_in, est_ref, joined_ref,
    recv, tap_all, jx, e0, e1, kx, za, zb, rt, yb, lg,
    a2a_s, a2a_r, own_sem, tap_s, tap_r, row_s, row_r, lo_s, lo_r, hi_s, hi_r, loc_sem,
    zs, zr, es, er, out_s, out_r,
):
    slabs, views, bands = dims
    strip = rows // views
    wide = strip + 2 * HALO
    margin = taps // 2
    z = lax.axis_index("gz")
    v = lax.axis_index("view")
    g = lax.axis_index("gy")

    def snake(band, place):
        return jnp.where(band % 2 == 1, views - 1 - place, place)

    idx = snake(g, v)
    me = g * views + idx
    strips = views * bands

    def dev(zz, vv, gg):
        return {"gz": zz, "view": vv, "gy": gg}

    def strip_dev(zz, ss):
        band = ss // views
        return dev(zz, snake(band, ss % views), band)

    below, above = z > 0, z < slabs - 1
    left, right = me > 0, me < strips - 1

    @pl.loop(0, views)
    def _(w):
        @pl.loop(0, 3 * CZ)
        def _(p):
            jx[w, p] = jnp.zeros((wide, 128), jnp.float32)

    @pl.loop(0, 3 * CZ)
    def _(p):
        e1[p] = jnp.zeros((wide, 128), jnp.float32)

    barrier = pltpu.get_barrier_semaphore()

    def greet(target):
        pl.semaphore_signal(barrier, inc=1, device_id=target, device_id_type=MESH)

    for d in range(1, slabs):
        greet(dev((z + d) % slabs, v, g))
    for d in range(1, strips):
        greet(strip_dev(z, (me + d) % strips))
    corners = []
    for dz, zok in ((-1, below), (1, above)):
        for ds, sok in ((-1, left), (1, right)):
            corners.append((dz, ds, zok & sok))
    amount = slabs - 1 + strips - 1
    for dz, ds, ok in corners:
        amount = amount + ok.astype(jnp.int32)

        @pl.when(ok)
        def _(dz=dz, ds=ds):
            greet(strip_dev(z + dz, me + ds))

    pl.semaphore_wait(barrier, amount)

    def a2a(d):
        to = (z + d) % slabs
        return pltpu.make_async_remote_copy(
            src_ref=acc_ref.at[to], dst_ref=recv.at[d - 1], send_sem=a2a_s.at[d - 1],
            recv_sem=a2a_r.at[d - 1], device_id=dev(to, v, g), device_id_type=MESH)

    for d in range(1, slabs):
        a2a(d).start()
    own = pltpu.make_async_copy(acc_ref.at[z], recv.at[slabs - 1], own_sem)
    own.start()
    own_tap = pltpu.make_async_copy(tap_in, tap_all.at[v], loc_sem.at[1])
    own_tap.start()

    def tap_copy(d):
        return pltpu.make_async_remote_copy(
            src_ref=tap_in, dst_ref=tap_all.at[v], send_sem=tap_s.at[d - 1],
            recv_sem=tap_r.at[d - 1], device_id={"view": (v + d) % views}, device_id_type=MESH)

    for d in range(1, views):
        tap_copy(d).start()
    own_tap.wait()
    for d in range(1, views):
        tap_copy(d).wait()

    apart = lax.broadcasted_iota(jnp.int32, (128, 128), 0) - lax.broadcasted_iota(jnp.int32, (128, 128), 1)

    @pl.loop(0, views)
    def _(w):
        ahead = jnp.zeros((128, 128), jnp.float32)
        back = jnp.zeros((128, 128), jnp.float32)
        for t in range(taps):
            tap = tap_all[w, 2 * taps + t : 2 * taps + t + 1, :]
            ahead = jnp.where(apart == t - margin, tap, ahead)
            back = jnp.where(apart == margin - t, tap, back)
        kx[w, 0] = ahead
        kx[w, 1] = back

    own.wait()
    for d in range(1, slabs):
        a2a(d).wait_recv()

    fy, fx = frac[1], frac[2]
    last_row = lax.broadcasted_iota(jnp.int32, (rows, 128), 0) == rows - 1
    last_col = lax.broadcasted_iota(jnp.int32, (rows, 128), 1) == 127

    @pl.loop(0, CZ)
    def _(p):
        at = pl.ds(pl.multiple_of(p * rows, 8), rows)
        cnt = pl.ds(CZ * rows + p, 1)
        total = recv[0, at, :]
        covered = recv[0, cnt, :]
        for s in range(1, slabs):
            total = total + recv[s, at, :]
            covered = covered + recv[s, cnt, :]
        follow = jnp.where(last_row, total, pltpu.roll(total, rows - 1, 0))
        total = (1.0 - fy) * total + fy * follow
        follow = jnp.where(last_col, total, pltpu.roll(total, 127, 1))
        total = (1.0 - fx) * total + fx * follow
        joined_ref[0, p] = jnp.maximum(total / (covered + 1.0), DATA_FLOOR)

    joined = joined_ref.at[0]
    mid = pl.ds(CZ, CZ)

    def main_piece(i):
        lo, hi = max(i * strip - HALO, 0), min((i + 1) * strip + HALO, rows)
        return pl.ds(lo, hi - lo), pl.ds(lo - i * strip + HALO, hi - lo)

    def main_copy(i, target, sem_at):
        src, dst = main_piece(i)
        return pltpu.make_async_remote_copy(
            src_ref=joined.at[:, src, :], dst_ref=jx.at[v, mid, dst, :], send_sem=row_s.at[i],
            recv_sem=row_r.at[sem_at], device_id={"view": target}, device_id_type=MESH)

    def main_local(i):
        src, dst = main_piece(i)
        return pltpu.make_async_copy(joined.at[:, src, :], jx.at[v, mid, dst, :], loc_sem.at[0])

    def edge_copy(up):
        src = pl.ds(rows - HALO, HALO) if up else pl.ds(0, HALO)
        dst = pl.ds(0, HALO) if up else pl.ds(HALO + strip, HALO)
        sems = (lo_s, lo_r) if up else (hi_s, hi_r)
        target = strip_dev(z, (g + 1) * views if up else g * views - 1)
        return pltpu.make_async_remote_copy(
            src_ref=joined.at[:, src, :], dst_ref=jx.at[v, mid, dst, :], send_sem=sems[0],
            recv_sem=sems[1].at[v], device_id=target, device_id_type=MESH)

    for i in range(views):
        owner = snake(g, i)

        @pl.when(owner != v)
        def _(i=i, owner=owner):
            main_copy(i, owner, v).start()

        @pl.when(owner == v)
        def _(i=i):
            main_local(i).start()

    next_band, prev_band = g < bands - 1, g > 0

    @pl.when(next_band)
    def _():
        edge_copy(True).start()

    @pl.when(prev_band)
    def _():
        edge_copy(False).start()

    def z_copy(w, up):
        dst = pl.ds(0, CZ) if up else pl.ds(2 * CZ, CZ)
        side = 1 if up else 0
        return pltpu.make_async_remote_copy(
            src_ref=jx.at[w, mid], dst_ref=jx.at[w, dst], send_sem=zs.at[side, w],
            recv_sem=zr.at[side, w], device_id={"gz": z + 1 if up else z - 1}, device_id_type=MESH)

    for d in range(views):
        w = (v + d) % views
        for i in range(views):
            if d == 0:
                @pl.when(idx == i)
                def _(i=i):
                    main_local(i).wait()
            else:
                @pl.when(idx == i)
                def _(i=i, w=w):
                    main_copy(i, v, w).wait_recv()

        @pl.when((idx == 0) & prev_band)
        def _(w=w):
            pltpu.make_async_remote_copy(
                src_ref=joined.at[:, pl.ds(rows - HALO, HALO), :], dst_ref=jx.at[w, mid, pl.ds(0, HALO), :],
                send_sem=lo_s, recv_sem=lo_r.at[w], device_id={"view": v}, device_id_type=MESH).wait_recv()

        @pl.when((idx == views - 1) & next_band)
        def _(w=w):
            pltpu.make_async_remote_copy(
                src_ref=joined.at[:, pl.ds(0, HALO), :], dst_ref=jx.at[w, mid, pl.ds(HALO + strip, HALO), :],
                send_sem=hi_s, recv_sem=hi_r.at[w], device_id={"view": v}, device_id_type=MESH).wait_recv()

        @pl.when(above)
        def _(w=w):
            z_copy(w, True).start()

        @pl.when(below)
        def _(w=w):
            z_copy(w, False).start()

    for d in range(views):
        w = (v + d) % views

        @pl.when(below)
        def _(w=w):
            z_copy(w, True).wait_recv()

        @pl.when(above)
        def _(w=w):
            z_copy(w, False).wait_recv()

    @pl.loop(0, 3 * CZ)
    def _(p):
        total = jx[0, p]
        for w in range(1, views):
            total = total + jx[w, p]
        e0[p] = total / views

    planes_r = CZ + 2 * margin
    rows_r = strip + 2 * margin

    def correct(est):
        for w in range(views):
            def tap(axis, t):
                at = axis * taps + t
                return tap_all[w, at : at + 1, :]

            @pl.loop(0, planes_r)
            def _(p):
                total = tap(0, 0) * est[p + CZ - 2 * margin]
                for t in range(1, taps):
                    total = total + tap(0, t) * est[p + CZ - 2 * margin + t]
                za[p] = total
                base = HALO - 2 * margin
                total = tap(1, 0) * za[p, base : base + rows_r, :]
                for t in range(1, taps):
                    total = total + tap(1, t) * za[p, base + t : base + t + rows_r, :]
                zb[p] = total

            @pl.loop(0, planes_r // 4)
            def _(c):
                at = pl.ds(c * 4, 4)
                blurred = jnp.dot(
                    zb[at].reshape(4 * rows_r, 128), kx[w, 0], precision=PRECISE,
                    preferred_element_type=jnp.float32).reshape(4, rows_r, 128)
                data = jx[w, pl.ds(c * 4 + CZ - margin, 4), HALO - margin : HALO - margin + rows_r, :]
                rt[at] = jnp.where(data > 0.0, data / blurred, 0.0)

            @pl.loop(0, CZ)
            def _(p):
                total = tap(0, taps - 1) * rt[p]
                for t in range(1, taps):
                    total = total + tap(0, taps - 1 - t) * rt[p + t]
                za[p, 0:rows_r, :] = total
                total = tap(1, taps - 1) * za[p, 0:strip, :]
                for t in range(1, taps):
                    total = total + tap(1, taps - 1 - t) * za[p, t : t + strip, :]
                yb[p] = total

            @pl.loop(0, CZ // 4)
            def _(c):
                at = pl.ds(c * 4, 4)
                logs = jnp.log(jnp.dot(
                    yb[at].reshape(4 * strip, 128), kx[w, 1], precision=PRECISE,
                    preferred_element_type=jnp.float32)).reshape(4, strip, 128)
                lg[at] = logs if w == 0 else lg[at] + logs

    inner = pl.ds(HALO, strip)
    near = []
    for n, (dz, ds) in enumerate([(a, b) for a in (-1, 0, 1) for b in (-1, 0, 1) if a or b]):
        zok = {-1: below, 0: z >= 0, 1: above}[dz]
        sok = {-1: left, 0: z >= 0, 1: right}[ds]
        far_z = {-1: above, 0: z >= 0, 1: below}[dz]
        far_s = {-1: right, 0: z >= 0, 1: left}[ds]
        near.append((n, dz, ds, zok & sok, far_z & far_s))

    def near_copy(n, dz, ds):
        src_r = {-1: pl.ds(HALO, HALO), 0: inner, 1: pl.ds(strip, HALO)}[ds]
        dst_r = {-1: pl.ds(HALO + strip, HALO), 0: inner, 1: pl.ds(0, HALO)}[ds]
        dst_p = {-1: pl.ds(2 * CZ, CZ), 0: mid, 1: pl.ds(0, CZ)}[dz]
        return pltpu.make_async_remote_copy(
            src_ref=e1.at[mid, src_r, :], dst_ref=e1.at[dst_p, dst_r, :], send_sem=es.at[n],
            recv_sem=er.at[n], device_id=strip_dev(z + dz, me + ds), device_id_type=MESH)

    def out_copy(target, sem_at):
        at = pl.ds(pl.multiple_of(idx * strip, 8), strip)
        return pltpu.make_async_remote_copy(
            src_ref=lg, dst_ref=est_ref.at[:, at, :], send_sem=out_s.at[sem_at],
            recv_sem=out_r.at[sem_at], device_id={"view": target}, device_id_type=MESH)

    correct(e0)
    for p in range(CZ):
        e1[CZ + p, inner, :] = e0[CZ + p, inner, :] * jnp.exp(lg[p] / views)
    for n, dz, ds, ok, _ in near:
        @pl.when(ok)
        def _(n=n, dz=dz, ds=ds):
            near_copy(n, dz, ds).start()
    for n, dz, ds, _, ok in near:
        @pl.when(ok)
        def _(n=n, dz=dz, ds=ds):
            near_copy(n, dz, ds).wait_recv()

    correct(e1)
    mine = pl.ds(pl.multiple_of(idx * strip, 8), strip)
    for p in range(CZ):
        done = e1[CZ + p, inner, :] * jnp.exp(lg[p] / views)
        lg[p] = done
        est_ref[p, mine, :] = done
    for d in range(1, views):
        out_copy((v + d) % views, d - 1).start()
    for d in range(1, views):
        out_copy((v + d) % views, d - 1).wait()

    for d in range(1, slabs):
        a2a(d).wait_send()
    for i in range(views):
        owner = snake(g, i)

        @pl.when(owner != v)
        def _(i=i, owner=owner):
            main_copy(i, owner, v).wait_send()

    @pl.when(next_band)
    def _():
        edge_copy(True).wait_send()

    @pl.when(prev_band)
    def _():
        edge_copy(False).wait_send()

    for w in range(views):
        @pl.when(above)
        def _(w=w):
            z_copy(w, True).wait_send()

        @pl.when(below)
        def _(w=w):
            z_copy(w, False).wait_send()

    for n, dz, ds, ok, _ in near:
        @pl.when(ok)
        def _(n=n, dz=dz, ds=ds):
            near_copy(n, dz, ds).wait_send()


def on_device(dims, camera, background, destination, offsets, shift_frac, psf_taps):
    slabs, views, bands = dims
    blocks, planes, rows, cols = camera.shape[1:]
    taps = psf_taps.shape[-1]
    margin = taps // 2
    tall = CZ * rows + CZ
    strip = rows // views
    wide = strip + 2 * HALO
    tap_rows = -(-3 * taps // 8) * 8
    smem = pl.BlockSpec(memory_space=pltpu.SMEM)
    acc, tap_rows_all = pl.pallas_call(
        functools.partial(deposit_kernel, rows),
        grid=(blocks // CHUNK,),
        in_specs=[smem] * 5 + [pl.BlockSpec((CHUNK, planes, rows, cols), lambda i: (i, 0, 0, 0))],
        out_specs=(
            pl.BlockSpec((slabs, tall, cols), lambda i: (0, 0, 0)),
            pl.BlockSpec((tap_rows, cols), lambda i: (0, 0)),
        ),
        out_shape=(
            jax.ShapeDtypeStruct((slabs, tall, cols), jnp.float32),
            jax.ShapeDtypeStruct((tap_rows, cols), jnp.float32),
        ),
        name="deposit",
    )(destination.reshape(-1), offsets.reshape(-1), background.reshape(-1), shift_frac[0], psf_taps[0], camera[0])

    vmem = pl.BlockSpec(memory_space=pltpu.VMEM)
    dma = pltpu.SemaphoreType.DMA
    f32 = jnp.float32
    estimate, joined = pl.pallas_call(
        functools.partial(world_kernel, dims, rows, taps),
        in_specs=[smem, pl.BlockSpec(memory_space=pl.ANY), vmem],
        out_specs=(vmem, vmem),
        out_shape=(
            jax.ShapeDtypeStruct((CZ, rows, cols), f32),
            jax.ShapeDtypeStruct((1, CZ, rows, cols), f32),
        ),
        scratch_shapes=[
            pltpu.VMEM((slabs, tall, cols), f32),
            pltpu.VMEM((views, tap_rows, cols), f32),
            pltpu.VMEM((views, 3 * CZ, wide, cols), f32),
            pltpu.VMEM((3 * CZ, wide, cols), f32),
            pltpu.VMEM((3 * CZ, wide, cols), f32),
            pltpu.VMEM((views, 2, cols, cols), f32),
            pltpu.VMEM((CZ + 2 * margin, wide, cols), f32),
            pltpu.VMEM((CZ + 2 * margin, strip + 2 * margin, cols), f32),
            pltpu.VMEM((CZ + 2 * margin, strip + 2 * margin, cols), f32),
            pltpu.VMEM((CZ, strip, cols), f32),
            pltpu.VMEM((CZ, strip, cols), f32),
            dma((slabs,)), dma((slabs,)), dma, dma((views,)), dma((views,)),
            dma((views,)), dma((views,)), dma, dma((views,)), dma, dma((views,)), dma((2,)),
            dma((2, views)), dma((2, views)), dma((8,)), dma((8,)), dma((views,)), dma((views,)),
        ],
        compiler_params=pltpu.CompilerParams(
            collective_id=0, has_side_effects=True, vmem_limit_bytes=40 * 1024 * 1024),
        name="world",
    )(shift_frac[0], acc, tap_rows_all)
    return estimate, joined


def solution(mesh):
    dims = (mesh.shape["gz"], mesh.shape["view"], mesh.shape["gy"])
    return jax.shard_map(
        functools.partial(on_device, dims),
        mesh=mesh,
        in_specs=(
            P("view", ("groups", "gz"), None, "gy", None),
            P("view", "gy", ("groups", "gz")),
            P("view", "gy", ("groups", "gz"), None),
            P("view", "gy", ("groups", "gz")),
            P("view", None),
            P("view", None, None),
        ),
        out_specs=(P(("groups", "gz"), "gy", None), P("view", ("groups", "gz"), "gy", None)),
        check_vma=False,
    )
```

```python
import functools

import jax
import jax.numpy as jnp
from jax import lax
from jax.experimental import pallas as pl
from jax.experimental.pallas import tpu as pltpu
from jax.sharding import PartitionSpec as P

CZ = 8
ITERS = 2
HALO = 8
CHUNK = 4

DATA_FLOOR = 0.25
MESH = pl.DeviceIdType.MESH


def deposit_kernel(
    rows, dest_ref, offs_ref, level_ref, frac_ref, psf_ref, cam_ref, acc_ref, tap_ref,
    dest, offs, level, frac, psf, cam, sems, small_sems,
):
    taps = psf_ref.shape[2]
    blocks, planes = cam_ref.shape[:2]

    def fetch(c):
        at = pl.ds(c * CHUNK, CHUNK)
        return pltpu.make_async_copy(cam_ref.at[at], cam.at[at], sems.at[c])

    small = [pltpu.make_async_copy(a, b, small_sems.at[n]) for n, (a, b) in enumerate(
        [(dest_ref, dest), (offs_ref, offs), (level_ref, level), (frac_ref, frac), (psf_ref, psf)])]
    for copy in small:
        copy.start()
    for c in range(blocks // CHUNK):
        fetch(c).start()

    @pl.loop(0, acc_ref.shape[0])
    def _(s):
        acc_ref[s] = jnp.zeros(acc_ref.shape[1:], jnp.float32)

    for copy in small:
        copy.wait()

    tap_ref[...] = jnp.zeros(tap_ref.shape, jnp.float32)
    for axis in range(3):
        scale = jnp.sum(psf[axis], axis=1, keepdims=True)
        share = psf[axis] / scale
        for t in range(taps):
            at = axis * taps + t
            tap_ref[at : at + 1, :] = jnp.broadcast_to(share[:, t : t + 1], (1, 128))

    fz = frac[0]
    base = level[0].astype(jnp.float32)

    @pl.loop(0, blocks // CHUNK)
    def _(c):
        fetch(c).wait()
        for i in range(CHUNK):
            b = c * CHUNK + i
            s = dest[b]
            o = offs[b]
            lower = cam[b, 0] - base
            for k in range(planes - 1):
                upper = cam[b, k + 1] - base
                at = pl.ds(pl.multiple_of((o + k) * rows, 8), rows)
                acc_ref[s, at, :] = acc_ref[s, at, :] + ((1.0 - fz) * lower + fz * upper)
                cnt = pl.ds(CZ * rows + o + k, 1)
                acc_ref[s, cnt, :] = acc_ref[s, cnt, :] + 1.0
                lower = upper


def world_kernel(
    dims, rows, taps,
    frac_ref, acc_ref, tap_in, est_ref, joined_ref,
    frac, up_in, down_in, tap_all, jx, e0, e1, kx, za, zb, rt, yb, lg,
    up_s, up_r, down_s, down_r, frac_sem, tap_s, tap_r, row_s, row_r, lo_s, lo_r, hi_s, hi_r, loc_sem,
    zs, zr, es, er, out_s, out_r,
):
    slabs, views, bands = dims
    strip = rows // views
    wide = strip + 2 * HALO
    margin = taps // 2
    z = lax.axis_index("gz")
    v = lax.axis_index("view")
    g = lax.axis_index("gy")

    def snake(band, place):
        return jnp.where(band % 2 == 1, views - 1 - place, place)

    idx = snake(g, v)
    me = g * views + idx
    strips = views * bands

    def dev(zz, vv, gg):
        return {"gz": zz, "view": vv, "gy": gg}

    def strip_dev(zz, ss):
        band = ss // views
        return dev(zz, snake(band, ss % views), band)

    below, above = z > 0, z < slabs - 1
    left, right = me > 0, me < strips - 1

    own_frac = pltpu.make_async_copy(frac_ref, frac, frac_sem)
    own_frac.start()

    @pl.loop(0, views)
    def _(w):
        @pl.loop(0, 3 * CZ)
        def _(p):
            jx[w, p] = jnp.zeros((wide, 128), jnp.float32)

    @pl.loop(0, 3 * CZ)
    def _(p):
        e1[p] = jnp.zeros((wide, 128), jnp.float32)

    barrier = pltpu.get_barrier_semaphore()

    def greet(target):
        pl.semaphore_signal(barrier, inc=1, device_id=target, device_id_type=MESH)

    for ok, dz in ((below, -1), (above, 1)):
        @pl.when(ok)
        def _(dz=dz):
            greet(dev(z + dz, v, g))

    for d in range(1, strips):
        greet(strip_dev(z, (me + d) % strips))
    corners = []
    for dz, zok in ((-1, below), (1, above)):
        for ds, sok in ((-1, left), (1, right)):
            corners.append((dz, ds, zok & sok))
    amount = strips - 1 + below.astype(jnp.int32) + above.astype(jnp.int32)
    for dz, ds, ok in corners:
        amount = amount + ok.astype(jnp.int32)

        @pl.when(ok)
        def _(dz=dz, ds=ds):
            greet(strip_dev(z + dz, me + ds))

    pl.semaphore_wait(barrier, amount)

    def relay(up, s, own):
        buf, sems = (up_in, (up_s, up_r)) if up else (down_in, (down_s, down_r))
        return pltpu.make_async_remote_copy(
            src_ref=acc_ref.at[s] if own else buf.at[s], dst_ref=buf.at[s], send_sem=sems[0].at[s],
            recv_sem=sems[1].at[s], device_id={"gz": z + 1 if up else z - 1}, device_id_type=MESH)

    ends = ((True, below, lambda s: z < s), (False, above, lambda s: z > s))
    up_order, down_order = list(range(slabs - 1, 0, -1)), list(range(slabs - 1))

    for s_up, s_down in zip(up_order, down_order):
        for (up, inner_device, passes), s in zip(ends, (s_up, s_down)):
            @pl.when(passes(s) & jnp.logical_not(inner_device))
            def _(up=up, s=s):
                relay(up, s, True).start()

    own_tap = pltpu.make_async_copy(tap_in, tap_all.at[v], loc_sem.at[1])
    own_tap.start()

    def tap_copy(d):
        return pltpu.make_async_remote_copy(
            src_ref=tap_in, dst_ref=tap_all.at[v], send_sem=tap_s.at[d - 1],
            recv_sem=tap_r.at[d - 1], device_id={"view": (v + d) % views}, device_id_type=MESH)

    for d in range(1, views):
        tap_copy(d).start()
    own_tap.wait()
    for d in range(1, views):
        tap_copy(d).wait()

    apart = lax.broadcasted_iota(jnp.int32, (128, 128), 0) - lax.broadcasted_iota(jnp.int32, (128, 128), 1)

    @pl.loop(0, views)
    def _(w):
        ahead = jnp.zeros((128, 128), jnp.float32)
        back = jnp.zeros((128, 128), jnp.float32)
        for t in range(taps):
            tap = tap_all[w, 2 * taps + t : 2 * taps + t + 1, :]
            ahead = jnp.where(apart == t - margin, tap, ahead)
            back = jnp.where(apart == margin - t, tap, back)
        for n, full in enumerate((ahead, back)):
            top = full.astype(jnp.bfloat16)
            kx[w, n, 0:128, 0:128] = top
            kx[w, n, 128:256, 0:128] = top
            kx[w, n, 0:128, 128:256] = (full - top.astype(jnp.float32)).astype(jnp.bfloat16)
            kx[w, n, 128:256, 128:256] = jnp.zeros((128, 128), jnp.bfloat16)

    for s_up, s_down in zip(up_order, down_order):
        for (up, inner_device, passes), s in zip(ends, (s_up, s_down)):
            @pl.when(passes(s) & inner_device)
            def _(up=up, s=s):
                buf = up_in if up else down_in
                relay(up, s, False).wait_recv()
                buf[s] = buf[s] + acc_ref[s]
                relay(up, s, False).start()

    @pl.when(below)
    def _():
        relay(True, z, False).wait_recv()

    @pl.when(above)
    def _():
        relay(False, z, False).wait_recv()

    own_frac.wait()
    fy, fx = frac[1], frac[2]
    last_row = lax.broadcasted_iota(jnp.int32, (rows, 128), 0) == rows - 1
    last_col = lax.broadcasted_iota(jnp.int32, (rows, 128), 1) == 127

    @pl.loop(0, CZ)
    def _(p):
        at = pl.ds(pl.multiple_of(p * rows, 8), rows)
        cnt = pl.ds(CZ * rows + p, 1)
        total = acc_ref[z, at, :]
        covered = acc_ref[z, cnt, :]
        for ok, buf in ((below, up_in), (above, down_in)):
            total = total + jnp.where(ok, buf[z, at, :], 0.0)
            covered = covered + jnp.where(ok, buf[z, cnt, :], 0.0)
        follow = jnp.where(last_row, total, pltpu.roll(total, rows - 1, 0))
        total = (1.0 - fy) * total + fy * follow
        follow = jnp.where(last_col, total, pltpu.roll(total, 127, 1))
        total = (1.0 - fx) * total + fx * follow
        joined_ref[0, p] = jnp.maximum(total / (covered + 1.0), DATA_FLOOR)

    joined = joined_ref.at[0]
    mid = pl.ds(CZ, CZ)

    def main_piece(i):
        lo, hi = max(i * strip - HALO, 0), min((i + 1) * strip + HALO, rows)
        return pl.ds(lo, hi - lo), pl.ds(lo - i * strip + HALO, hi - lo)

    def main_copy(i, target, sem_at):
        src, dst = main_piece(i)
        return pltpu.make_async_remote_copy(
            src_ref=joined.at[:, src, :], dst_ref=jx.at[v, mid, dst, :], send_sem=row_s.at[i],
            recv_sem=row_r.at[sem_at], device_id={"view": target}, device_id_type=MESH)

    def main_local(i):
        src, dst = main_piece(i)
        return pltpu.make_async_copy(joined.at[:, src, :], jx.at[v, mid, dst, :], loc_sem.at[0])

    def edge_copy(up):
        src = pl.ds(rows - HALO, HALO) if up else pl.ds(0, HALO)
        dst = pl.ds(0, HALO) if up else pl.ds(HALO + strip, HALO)
        sems = (lo_s, lo_r) if up else (hi_s, hi_r)
        target = strip_dev(z, (g + 1) * views if up else g * views - 1)
        return pltpu.make_async_remote_copy(
            src_ref=joined.at[:, src, :], dst_ref=jx.at[v, mid, dst, :], send_sem=sems[0],
            recv_sem=sems[1].at[v], device_id=target, device_id_type=MESH)

    for i in range(views):
        owner = snake(g, i)

        @pl.when(owner != v)
        def _(i=i, owner=owner):
            main_copy(i, owner, v).start()

        @pl.when(owner == v)
        def _(i=i):
            main_local(i).start()

    next_band, prev_band = g < bands - 1, g > 0

    @pl.when(next_band)
    def _():
        edge_copy(True).start()

    @pl.when(prev_band)
    def _():
        edge_copy(False).start()

    def z_copy(w, up):
        dst = pl.ds(0, CZ) if up else pl.ds(2 * CZ, CZ)
        side = 1 if up else 0
        return pltpu.make_async_remote_copy(
            src_ref=jx.at[w, mid], dst_ref=jx.at[w, dst], send_sem=zs.at[side, w],
            recv_sem=zr.at[side, w], device_id={"gz": z + 1 if up else z - 1}, device_id_type=MESH)

    for d in range(views):
        w = (v + d) % views
        for i in range(views):
            if d == 0:
                @pl.when(idx == i)
                def _(i=i):
                    main_local(i).wait()
            else:
                @pl.when(idx == i)
                def _(i=i, w=w):
                    main_copy(i, v, w).wait_recv()

        @pl.when((idx == 0) & prev_band)
        def _(w=w):
            pltpu.make_async_remote_copy(
                src_ref=joined.at[:, pl.ds(rows - HALO, HALO), :], dst_ref=jx.at[w, mid, pl.ds(0, HALO), :],
                send_sem=lo_s, recv_sem=lo_r.at[w], device_id={"view": v}, device_id_type=MESH).wait_recv()

        @pl.when((idx == views - 1) & next_band)
        def _(w=w):
            pltpu.make_async_remote_copy(
                src_ref=joined.at[:, pl.ds(0, HALO), :], dst_ref=jx.at[w, mid, pl.ds(HALO + strip, HALO), :],
                send_sem=hi_s, recv_sem=hi_r.at[w], device_id={"view": v}, device_id_type=MESH).wait_recv()

        @pl.when(above)
        def _(w=w):
            z_copy(w, True).start()

        @pl.when(below)
        def _(w=w):
            z_copy(w, False).start()

    for d in range(views):
        w = (v + d) % views

        @pl.when(below)
        def _(w=w):
            z_copy(w, True).wait_recv()

        @pl.when(above)
        def _(w=w):
            z_copy(w, False).wait_recv()

    @pl.loop(0, 3 * CZ)
    def _(p):
        total = jx[0, p]
        for w in range(1, views):
            total = total + jx[w, p]
        e0[p] = total / views

    planes_r = CZ + 2 * margin
    rows_r = strip + 2 * margin

    def along_x(u, w, n):
        top = u.astype(jnp.bfloat16)
        rest = (u - top.astype(jnp.float32)).astype(jnp.bfloat16)
        both = jnp.dot(jnp.concatenate([top, rest], axis=1), kx[w, n], preferred_element_type=jnp.float32)
        return both[:, 0:128] + both[:, 128:256]

    def weighted(terms, weights):
        total = weights[0] * terms[0]
        for term, weight in zip(terms[1:], weights[1:]):
            total = total + weight * term
        return total

    def correct(est):
        for w in range(views):
            def tap(axis, t):
                at = axis * taps + t
                return tap_all[w, at : at + 1, :]

            @pl.loop(0, wide // 8, unroll=2)
            def _(r):
                at = pl.ds(pl.multiple_of(r * 8, 8), 8)
                column = [est[CZ - 2 * margin + p, at, :] for p in range(planes_r + 2 * margin)]
                for p in range(planes_r):
                    za[p, at, :] = weighted(column[p : p + taps], [tap(0, t) for t in range(taps)])

            @pl.loop(0, planes_r, unroll=4)
            def _(p):
                base = HALO - 2 * margin
                zb[p] = weighted([za[p, base + t : base + t + rows_r, :] for t in range(taps)],
                                 [tap(1, t) for t in range(taps)])

            @pl.loop(0, planes_r // 4)
            def _(c):
                at = pl.ds(c * 4, 4)
                blurred = along_x(zb[at].reshape(4 * rows_r, 128), w, 0).reshape(4, rows_r, 128)
                data = jx[w, pl.ds(c * 4 + CZ - margin, 4), HALO - margin : HALO - margin + rows_r, :]
                rt[at] = jnp.where(data > 0.0, data / blurred, 0.0)

            @pl.loop(0, rows_r // 8, unroll=True)
            def _(r):
                at = pl.ds(pl.multiple_of(r * 8, 8), 8)
                column = [rt[p, at, :] for p in range(planes_r)]
                for p in range(CZ):
                    za[p, at, :] = weighted(column[p : p + taps], [tap(0, taps - 1 - t) for t in range(taps)])

            @pl.loop(0, CZ, unroll=4)
            def _(p):
                yb[p] = weighted([za[p, t : t + strip, :] for t in range(taps)],
                                 [tap(1, taps - 1 - t) for t in range(taps)])

            @pl.loop(0, CZ // 4)
            def _(c):
                at = pl.ds(c * 4, 4)
                logs = jnp.log(along_x(yb[at].reshape(4 * strip, 128), w, 1)).reshape(4, strip, 128)
                lg[at] = logs if w == 0 else lg[at] + logs

    inner = pl.ds(HALO, strip)
    near = []
    for n, (dz, ds) in enumerate([(a, b) for a in (-1, 0, 1) for b in (-1, 0, 1) if a or b]):
        zok = {-1: below, 0: z >= 0, 1: above}[dz]
        sok = {-1: left, 0: z >= 0, 1: right}[ds]
        far_z = {-1: above, 0: z >= 0, 1: below}[dz]
        far_s = {-1: right, 0: z >= 0, 1: left}[ds]
        near.append((n, dz, ds, zok & sok, far_z & far_s))

    def near_copy(n, dz, ds):
        src_r = {-1: pl.ds(HALO, HALO), 0: inner, 1: pl.ds(strip, HALO)}[ds]
        dst_r = {-1: pl.ds(HALO + strip, HALO), 0: inner, 1: pl.ds(0, HALO)}[ds]
        dst_p = {-1: pl.ds(2 * CZ, CZ), 0: mid, 1: pl.ds(0, CZ)}[dz]
        return pltpu.make_async_remote_copy(
            src_ref=e1.at[mid, src_r, :], dst_ref=e1.at[dst_p, dst_r, :], send_sem=es.at[n],
            recv_sem=er.at[n], device_id=strip_dev(z + dz, me + ds), device_id_type=MESH)

    def out_copy(target, sem_at):
        at = pl.ds(pl.multiple_of(idx * strip, 8), strip)
        return pltpu.make_async_remote_copy(
            src_ref=lg, dst_ref=est_ref.at[:, at, :], send_sem=out_s.at[sem_at],
            recv_sem=out_r.at[sem_at], device_id={"view": target}, device_id_type=MESH)

    correct(e0)
    for p in range(CZ):
        e1[CZ + p, inner, :] = e0[CZ + p, inner, :] * jnp.exp(lg[p] / views)
    for n, dz, ds, ok, _ in near:
        @pl.when(ok)
        def _(n=n, dz=dz, ds=ds):
            near_copy(n, dz, ds).start()
    for n, dz, ds, _, ok in near:
        @pl.when(ok)
        def _(n=n, dz=dz, ds=ds):
            near_copy(n, dz, ds).wait_recv()

    correct(e1)
    mine = pl.ds(pl.multiple_of(idx * strip, 8), strip)
    for p in range(CZ):
        done = e1[CZ + p, inner, :] * jnp.exp(lg[p] / views)
        lg[p] = done
        est_ref[p, mine, :] = done
    for d in range(1, views):
        out_copy((v + d) % views, d - 1).start()
    for d in range(1, views):
        out_copy((v + d) % views, d - 1).wait()

    for s_up, s_down in zip(up_order, down_order):
        for (up, _, passes), s in zip(ends, (s_up, s_down)):
            @pl.when(passes(s))
            def _(up=up, s=s):
                relay(up, s, False).wait_send()

    for i in range(views):
        owner = snake(g, i)

        @pl.when(owner != v)
        def _(i=i, owner=owner):
            main_copy(i, owner, v).wait_send()

    @pl.when(next_band)
    def _():
        edge_copy(True).wait_send()

    @pl.when(prev_band)
    def _():
        edge_copy(False).wait_send()

    for w in range(views):
        @pl.when(above)
        def _(w=w):
            z_copy(w, True).wait_send()

        @pl.when(below)
        def _(w=w):
            z_copy(w, False).wait_send()

    for n, dz, ds, ok, _ in near:
        @pl.when(ok)
        def _(n=n, dz=dz, ds=ds):
            near_copy(n, dz, ds).wait_send()


def on_device(dims, camera, background, destination, offsets, shift_frac, psf_taps):
    slabs, views, bands = dims
    blocks, planes, rows, cols = camera.shape[1:]
    taps = psf_taps.shape[-1]
    margin = taps // 2
    tall = CZ * rows + CZ
    strip = rows // views
    wide = strip + 2 * HALO
    tap_rows = -(-3 * taps // 8) * 8
    vmem = pl.BlockSpec(memory_space=pltpu.VMEM)
    hbm = pl.BlockSpec(memory_space=pltpu.HBM)
    acc, tap_rows_all = pl.pallas_call(
        functools.partial(deposit_kernel, rows),
        in_specs=[hbm] * 6,
        out_specs=(vmem, vmem),
        out_shape=(
            jax.ShapeDtypeStruct((slabs, tall, cols), jnp.float32),
            jax.ShapeDtypeStruct((tap_rows, cols), jnp.float32),
        ),
        scratch_shapes=[
            pltpu.SMEM((blocks,), jnp.int32),
            pltpu.SMEM((blocks,), jnp.int32),
            pltpu.SMEM((1,), jnp.int32),
            pltpu.SMEM((3,), jnp.float32),
            pltpu.VMEM((3, 1, taps), jnp.float32),
            pltpu.VMEM((blocks, planes, rows, cols), jnp.float32),
            pltpu.SemaphoreType.DMA((blocks // CHUNK,)),
            pltpu.SemaphoreType.DMA((5,)),
        ],
        compiler_params=pltpu.CompilerParams(vmem_limit_bytes=60 * 1024 * 1024),
        name="deposit",
    )(destination.reshape(-1), offsets.reshape(-1), background.reshape(-1), shift_frac[0], jnp.transpose(psf_taps, (1, 0, 2)), camera[0])

    dma = pltpu.SemaphoreType.DMA
    f32 = jnp.float32
    estimate, joined = pl.pallas_call(
        functools.partial(world_kernel, dims, rows, taps),
        in_specs=[hbm, vmem, vmem],
        out_specs=(vmem, vmem),
        out_shape=(
            jax.ShapeDtypeStruct((CZ, rows, cols), f32),
            jax.ShapeDtypeStruct((1, CZ, rows, cols), f32),
        ),
        scratch_shapes=[
            pltpu.SMEM((3,), f32),
            pltpu.VMEM((slabs, tall, cols), f32),
            pltpu.VMEM((slabs, tall, cols), f32),
            pltpu.VMEM((views, tap_rows, cols), f32),
            pltpu.VMEM((views, 3 * CZ, wide, cols), f32),
            pltpu.VMEM((3 * CZ, wide, cols), f32),
            pltpu.VMEM((3 * CZ, wide, cols), f32),
            pltpu.VMEM((views, 2, 2 * cols, 2 * cols), jnp.bfloat16),
            pltpu.VMEM((CZ + 2 * margin, wide, cols), f32),
            pltpu.VMEM((CZ + 2 * margin, strip + 2 * margin, cols), f32),
            pltpu.VMEM((CZ + 2 * margin, strip + 2 * margin, cols), f32),
            pltpu.VMEM((CZ, strip, cols), f32),
            pltpu.VMEM((CZ, strip, cols), f32),
            dma((slabs,)), dma((slabs,)), dma((slabs,)), dma((slabs,)), dma, dma((views,)), dma((views,)),
            dma((views,)), dma((views,)), dma, dma((views,)), dma, dma((views,)), dma((2,)),
            dma((2, views)), dma((2, views)), dma((8,)), dma((8,)), dma((views,)), dma((views,)),
        ],
        compiler_params=pltpu.CompilerParams(
            collective_id=0, has_side_effects=True, vmem_limit_bytes=58 * 1024 * 1024),
        name="world",
    )(shift_frac[0], acc, tap_rows_all)
    return estimate, joined


def solution(mesh):
    dims = (mesh.shape["gz"], mesh.shape["view"], mesh.shape["gy"])
    return jax.shard_map(
        functools.partial(on_device, dims),
        mesh=mesh,
        in_specs=(
            P("view", ("groups", "gz"), None, "gy", None),
            P("view", "gy", ("groups", "gz")),
            P("view", "gy", ("groups", "gz"), None),
            P("view", "gy", ("groups", "gz")),
            P("view", None),
            P("view", None, None),
        ),
        out_specs=(P(("groups", "gz"), "gy", None), P("view", ("groups", "gz"), "gy", None)),
        check_vma=False,
    )
```

```python
import functools

import jax
import jax.numpy as jnp
from jax import lax
from jax.experimental import pallas as pl
from jax.experimental.pallas import tpu as pltpu
from jax.sharding import PartitionSpec as P

CZ = 8
ITERS = 2
HALO = 8
CHUNK = 4

DATA_FLOOR = 0.25
MESH = pl.DeviceIdType.MESH


def deposit_kernel(rows, dest, offs, level, frac, psf, cam_ref, acc_ref, tap_ref, cam, sems):
    taps = psf.shape[2]
    blocks, planes = cam_ref.shape[:2]

    def fetch(c):
        at = pl.ds(c * CHUNK, CHUNK)
        return pltpu.make_async_copy(cam_ref.at[at], cam.at[at], sems.at[c])

    for c in range(blocks // CHUNK):
        fetch(c).start()

    @pl.loop(0, acc_ref.shape[0])
    def _(s):
        acc_ref[s] = jnp.zeros(acc_ref.shape[1:], jnp.float32)

    tap_ref[...] = jnp.zeros(tap_ref.shape, jnp.float32)
    for axis in range(3):
        scale = jnp.sum(psf[axis], axis=1, keepdims=True)
        share = psf[axis] / scale
        for t in range(taps):
            at = axis * taps + t
            tap_ref[at : at + 1, :] = jnp.broadcast_to(share[:, t : t + 1], (1, 128))

    fz = frac[0]
    base = level[0].astype(jnp.float32)

    @pl.loop(0, blocks // CHUNK)
    def _(c):
        fetch(c).wait()
        for i in range(CHUNK):
            b = c * CHUNK + i
            s = dest[b]
            o = offs[b]
            lower = cam[b, 0] - base
            for k in range(planes - 1):
                upper = cam[b, k + 1] - base
                at = pl.ds(pl.multiple_of((o + k) * rows, 8), rows)
                acc_ref[s, at, :] = acc_ref[s, at, :] + ((1.0 - fz) * lower + fz * upper)
                cnt = pl.ds(CZ * rows + o + k, 1)
                acc_ref[s, cnt, :] = acc_ref[s, cnt, :] + 1.0
                lower = upper


def world_kernel(
    dims, rows, taps,
    frac, acc_ref, tap_in, est_ref, joined_ref,
    recv, tap_all, jx, e0, e1, kx, za, zb, rt, yb, lg,
    a2a_s, a2a_r, own_sem, tap_s, tap_r, row_s, row_r, lo_s, lo_r, hi_s, hi_r, loc_sem,
    zs, zr, es, er, out_s, out_r,
):
    slabs, views, bands = dims
    strip = rows // views
    wide = strip + 2 * HALO
    margin = taps // 2
    z = lax.axis_index("gz")
    v = lax.axis_index("view")
    g = lax.axis_index("gy")

    def snake(band, place):
        return jnp.where(band % 2 == 1, views - 1 - place, place)

    idx = snake(g, v)
    me = g * views + idx
    strips = views * bands

    def dev(zz, vv, gg):
        return {"gz": zz, "view": vv, "gy": gg}

    def strip_dev(zz, ss):
        band = ss // views
        return dev(zz, snake(band, ss % views), band)

    below, above = z > 0, z < slabs - 1
    left, right = me > 0, me < strips - 1

    @pl.loop(0, views)
    def _(w):
        @pl.loop(0, 3 * CZ)
        def _(p):
            jx[w, p] = jnp.zeros((wide, 128), jnp.float32)

    @pl.loop(0, 3 * CZ)
    def _(p):
        e1[p] = jnp.zeros((wide, 128), jnp.float32)

    barrier = pltpu.get_barrier_semaphore()

    def greet(target):
        pl.semaphore_signal(barrier, inc=1, device_id=target, device_id_type=MESH)

    for d in range(1, slabs):
        greet(dev((z + d) % slabs, v, g))
    for d in range(1, strips):
        greet(strip_dev(z, (me + d) % strips))
    corners = []
    for dz, zok in ((-1, below), (1, above)):
        for ds, sok in ((-1, left), (1, right)):
            corners.append((dz, ds, zok & sok))
    amount = slabs - 1 + strips - 1
    for dz, ds, ok in corners:
        amount = amount + ok.astype(jnp.int32)

        @pl.when(ok)
        def _(dz=dz, ds=ds):
            greet(strip_dev(z + dz, me + ds))

    pl.semaphore_wait(barrier, amount)

    def a2a(d):
        to = (z + d) % slabs
        return pltpu.make_async_remote_copy(
            src_ref=acc_ref.at[to], dst_ref=recv.at[d - 1], send_sem=a2a_s.at[d - 1],
            recv_sem=a2a_r.at[d - 1], device_id=dev(to, v, g), device_id_type=MESH)

    for d in range(1, slabs):
        a2a(d).start()
    own = pltpu.make_async_copy(acc_ref.at[z], recv.at[slabs - 1], own_sem)
    own.start()
    own_tap = pltpu.make_async_copy(tap_in, tap_all.at[v], loc_sem.at[1])
    own_tap.start()

    def tap_copy(d):
        return pltpu.make_async_remote_copy(
            src_ref=tap_in, dst_ref=tap_all.at[v], send_sem=tap_s.at[d - 1],
            recv_sem=tap_r.at[d - 1], device_id={"view": (v + d) % views}, device_id_type=MESH)

    for d in range(1, views):
        tap_copy(d).start()
    own_tap.wait()
    for d in range(1, views):
        tap_copy(d).wait()

    apart = lax.broadcasted_iota(jnp.int32, (128, 128), 0) - lax.broadcasted_iota(jnp.int32, (128, 128), 1)

    @pl.loop(0, views)
    def _(w):
        ahead = jnp.zeros((128, 128), jnp.float32)
        back = jnp.zeros((128, 128), jnp.float32)
        for t in range(taps):
            tap = tap_all[w, 2 * taps + t : 2 * taps + t + 1, :]
            ahead = jnp.where(apart == t - margin, tap, ahead)
            back = jnp.where(apart == margin - t, tap, back)
        for n, full in enumerate((ahead, back)):
            top = full.astype(jnp.bfloat16)
            kx[w, n, 0:128, 0:128] = top
            kx[w, n, 128:256, 0:128] = top
            kx[w, n, 0:128, 128:256] = (full - top.astype(jnp.float32)).astype(jnp.bfloat16)
            kx[w, n, 128:256, 128:256] = jnp.zeros((128, 128), jnp.bfloat16)

    own.wait()
    for d in range(1, slabs):
        a2a(d).wait_recv()

    fy, fx = frac[1], frac[2]
    last_row = lax.broadcasted_iota(jnp.int32, (rows, 128), 0) == rows - 1
    last_col = lax.broadcasted_iota(jnp.int32, (rows, 128), 1) == 127

    @pl.loop(0, CZ)
    def _(p):
        at = pl.ds(pl.multiple_of(p * rows, 8), rows)
        cnt = pl.ds(CZ * rows + p, 1)
        total = recv[0, at, :]
        covered = recv[0, cnt, :]
        for s in range(1, slabs):
            total = total + recv[s, at, :]
            covered = covered + recv[s, cnt, :]
        follow = jnp.where(last_row, total, pltpu.roll(total, rows - 1, 0))
        total = (1.0 - fy) * total + fy * follow
        follow = jnp.where(last_col, total, pltpu.roll(total, 127, 1))
        total = (1.0 - fx) * total + fx * follow
        joined_ref[0, p] = jnp.maximum(total / (covered + 1.0), DATA_FLOOR)

    joined = joined_ref.at[0]
    mid = pl.ds(CZ, CZ)

    def main_piece(i):
        lo, hi = max(i * strip - HALO, 0), min((i + 1) * strip + HALO, rows)
        return pl.ds(lo, hi - lo), pl.ds(lo - i * strip + HALO, hi - lo)

    def main_copy(i, target, sem_at):
        src, dst = main_piece(i)
        return pltpu.make_async_remote_copy(
            src_ref=joined.at[:, src, :], dst_ref=jx.at[v, mid, dst, :], send_sem=row_s.at[i],
            recv_sem=row_r.at[sem_at], device_id={"view": target}, device_id_type=MESH)

    def main_local(i):
        src, dst = main_piece(i)
        return pltpu.make_async_copy(joined.at[:, src, :], jx.at[v, mid, dst, :], loc_sem.at[0])

    def edge_copy(up):
        src = pl.ds(rows - HALO, HALO) if up else pl.ds(0, HALO)
        dst = pl.ds(0, HALO) if up else pl.ds(HALO + strip, HALO)
        sems = (lo_s, lo_r) if up else (hi_s, hi_r)
        target = strip_dev(z, (g + 1) * views if up else g * views - 1)
        return pltpu.make_async_remote_copy(
            src_ref=joined.at[:, src, :], dst_ref=jx.at[v, mid, dst, :], send_sem=sems[0],
            recv_sem=sems[1].at[v], device_id=target, device_id_type=MESH)

    for i in range(views):
        owner = snake(g, i)

        @pl.when(owner != v)
        def _(i=i, owner=owner):
            main_copy(i, owner, v).start()

        @pl.when(owner == v)
        def _(i=i):
            main_local(i).start()

    next_band, prev_band = g < bands - 1, g > 0

    @pl.when(next_band)
    def _():
        edge_copy(True).start()

    @pl.when(prev_band)
    def _():
        edge_copy(False).start()

    def z_copy(w, up):
        dst = pl.ds(0, CZ) if up else pl.ds(2 * CZ, CZ)
        side = 1 if up else 0
        return pltpu.make_async_remote_copy(
            src_ref=jx.at[w, mid], dst_ref=jx.at[w, dst], send_sem=zs.at[side, w],
            recv_sem=zr.at[side, w], device_id={"gz": z + 1 if up else z - 1}, device_id_type=MESH)

    for d in range(views):
        w = (v + d) % views
        for i in range(views):
            if d == 0:
                @pl.when(idx == i)
                def _(i=i):
                    main_local(i).wait()
            else:
                @pl.when(idx == i)
                def _(i=i, w=w):
                    main_copy(i, v, w).wait_recv()

        @pl.when((idx == 0) & prev_band)
        def _(w=w):
            pltpu.make_async_remote_copy(
                src_ref=joined.at[:, pl.ds(rows - HALO, HALO), :], dst_ref=jx.at[w, mid, pl.ds(0, HALO), :],
                send_sem=lo_s, recv_sem=lo_r.at[w], device_id={"view": v}, device_id_type=MESH).wait_recv()

        @pl.when((idx == views - 1) & next_band)
        def _(w=w):
            pltpu.make_async_remote_copy(
                src_ref=joined.at[:, pl.ds(0, HALO), :], dst_ref=jx.at[w, mid, pl.ds(HALO + strip, HALO), :],
                send_sem=hi_s, recv_sem=hi_r.at[w], device_id={"view": v}, device_id_type=MESH).wait_recv()

        @pl.when(above)
        def _(w=w):
            z_copy(w, True).start()

        @pl.when(below)
        def _(w=w):
            z_copy(w, False).start()

    for d in range(views):
        w = (v + d) % views

        @pl.when(below)
        def _(w=w):
            z_copy(w, True).wait_recv()

        @pl.when(above)
        def _(w=w):
            z_copy(w, False).wait_recv()

    @pl.loop(0, 3 * CZ)
    def _(p):
        total = jx[0, p]
        for w in range(1, views):
            total = total + jx[w, p]
        e0[p] = total / views

    planes_r = CZ + 2 * margin
    rows_r = strip + 2 * margin

    def along_x(u, w, n):
        top = u.astype(jnp.bfloat16)
        rest = (u - top.astype(jnp.float32)).astype(jnp.bfloat16)
        both = jnp.dot(jnp.concatenate([top, rest], axis=1), kx[w, n], preferred_element_type=jnp.float32)
        return both[:, 0:128] + both[:, 128:256]

    def weighted(terms, weights):
        total = weights[0] * terms[0]
        for term, weight in zip(terms[1:], weights[1:]):
            total = total + weight * term
        return total

    def correct(est):
        for w in range(views):
            def tap(axis, t):
                at = axis * taps + t
                return tap_all[w, at : at + 1, :]

            @pl.loop(0, wide // 8, unroll=2)
            def _(r):
                at = pl.ds(pl.multiple_of(r * 8, 8), 8)
                column = [est[CZ - 2 * margin + p, at, :] for p in range(planes_r + 2 * margin)]
                for p in range(planes_r):
                    za[p, at, :] = weighted(column[p : p + taps], [tap(0, t) for t in range(taps)])

            @pl.loop(0, planes_r, unroll=4)
            def _(p):
                base = HALO - 2 * margin
                zb[p] = weighted([za[p, base + t : base + t + rows_r, :] for t in range(taps)],
                                 [tap(1, t) for t in range(taps)])

            @pl.loop(0, planes_r // 4)
            def _(c):
                at = pl.ds(c * 4, 4)
                blurred = along_x(zb[at].reshape(4 * rows_r, 128), w, 0).reshape(4, rows_r, 128)
                data = jx[w, pl.ds(c * 4 + CZ - margin, 4), HALO - margin : HALO - margin + rows_r, :]
                rt[at] = jnp.where(data > 0.0, data / blurred, 0.0)

            @pl.loop(0, rows_r // 8, unroll=True)
            def _(r):
                at = pl.ds(pl.multiple_of(r * 8, 8), 8)
                column = [rt[p, at, :] for p in range(planes_r)]
                for p in range(CZ):
                    za[p, at, :] = weighted(column[p : p + taps], [tap(0, taps - 1 - t) for t in range(taps)])

            @pl.loop(0, CZ, unroll=4)
            def _(p):
                yb[p] = weighted([za[p, t : t + strip, :] for t in range(taps)],
                                 [tap(1, taps - 1 - t) for t in range(taps)])

            @pl.loop(0, CZ // 4)
            def _(c):
                at = pl.ds(c * 4, 4)
                logs = jnp.log(along_x(yb[at].reshape(4 * strip, 128), w, 1)).reshape(4, strip, 128)
                lg[at] = logs if w == 0 else lg[at] + logs

    inner = pl.ds(HALO, strip)
    near = []
    for n, (dz, ds) in enumerate([(a, b) for a in (-1, 0, 1) for b in (-1, 0, 1) if a or b]):
        zok = {-1: below, 0: z >= 0, 1: above}[dz]
        sok = {-1: left, 0: z >= 0, 1: right}[ds]
        far_z = {-1: above, 0: z >= 0, 1: below}[dz]
        far_s = {-1: right, 0: z >= 0, 1: left}[ds]
        near.append((n, dz, ds, zok & sok, far_z & far_s))

    def near_copy(n, dz, ds):
        src_r = {-1: pl.ds(HALO, HALO), 0: inner, 1: pl.ds(strip, HALO)}[ds]
        dst_r = {-1: pl.ds(HALO + strip, HALO), 0: inner, 1: pl.ds(0, HALO)}[ds]
        dst_p = {-1: pl.ds(2 * CZ, CZ), 0: mid, 1: pl.ds(0, CZ)}[dz]
        return pltpu.make_async_remote_copy(
            src_ref=e1.at[mid, src_r, :], dst_ref=e1.at[dst_p, dst_r, :], send_sem=es.at[n],
            recv_sem=er.at[n], device_id=strip_dev(z + dz, me + ds), device_id_type=MESH)

    def out_copy(target, sem_at):
        at = pl.ds(pl.multiple_of(idx * strip, 8), strip)
        return pltpu.make_async_remote_copy(
            src_ref=lg, dst_ref=est_ref.at[:, at, :], send_sem=out_s.at[sem_at],
            recv_sem=out_r.at[sem_at], device_id={"view": target}, device_id_type=MESH)

    correct(e0)
    for p in range(CZ):
        e1[CZ + p, inner, :] = e0[CZ + p, inner, :] * jnp.exp(lg[p] / views)
    for n, dz, ds, ok, _ in near:
        @pl.when(ok)
        def _(n=n, dz=dz, ds=ds):
            near_copy(n, dz, ds).start()
    for n, dz, ds, _, ok in near:
        @pl.when(ok)
        def _(n=n, dz=dz, ds=ds):
            near_copy(n, dz, ds).wait_recv()

    correct(e1)
    mine = pl.ds(pl.multiple_of(idx * strip, 8), strip)
    for p in range(CZ):
        done = e1[CZ + p, inner, :] * jnp.exp(lg[p] / views)
        lg[p] = done
        est_ref[p, mine, :] = done
    for d in range(1, views):
        out_copy((v + d) % views, d - 1).start()
    for d in range(1, views):
        out_copy((v + d) % views, d - 1).wait()

    for d in range(1, slabs):
        a2a(d).wait_send()
    for i in range(views):
        owner = snake(g, i)

        @pl.when(owner != v)
        def _(i=i, owner=owner):
            main_copy(i, owner, v).wait_send()

    @pl.when(next_band)
    def _():
        edge_copy(True).wait_send()

    @pl.when(prev_band)
    def _():
        edge_copy(False).wait_send()

    for w in range(views):
        @pl.when(above)
        def _(w=w):
            z_copy(w, True).wait_send()

        @pl.when(below)
        def _(w=w):
            z_copy(w, False).wait_send()

    for n, dz, ds, ok, _ in near:
        @pl.when(ok)
        def _(n=n, dz=dz, ds=ds):
            near_copy(n, dz, ds).wait_send()


def on_device(dims, camera, background, destination, offsets, shift_frac, psf_taps):
    slabs, views, bands = dims
    blocks, planes, rows, cols = camera.shape[1:]
    taps = psf_taps.shape[-1]
    margin = taps // 2
    tall = CZ * rows + CZ
    strip = rows // views
    wide = strip + 2 * HALO
    tap_rows = -(-3 * taps // 8) * 8
    smem = pl.BlockSpec(memory_space=pltpu.SMEM)
    vmem = pl.BlockSpec(memory_space=pltpu.VMEM)
    acc, tap_rows_all = pl.pallas_call(
        functools.partial(deposit_kernel, rows),
        in_specs=[smem] * 4 + [vmem, pl.BlockSpec(memory_space=pl.ANY)],
        out_specs=(vmem, vmem),
        out_shape=(
            jax.ShapeDtypeStruct((slabs, tall, cols), jnp.float32),
            jax.ShapeDtypeStruct((tap_rows, cols), jnp.float32),
        ),
        scratch_shapes=[
            pltpu.VMEM((blocks, planes, rows, cols), jnp.float32),
            pltpu.SemaphoreType.DMA((blocks // CHUNK,)),
        ],
        compiler_params=pltpu.CompilerParams(vmem_limit_bytes=60 * 1024 * 1024),
        name="deposit",
    )(destination.reshape(-1), offsets.reshape(-1), background.reshape(-1), shift_frac[0], jnp.transpose(psf_taps, (1, 0, 2)), camera[0])

    dma = pltpu.SemaphoreType.DMA
    f32 = jnp.float32
    estimate, joined = pl.pallas_call(
        functools.partial(world_kernel, dims, rows, taps),
        in_specs=[smem, vmem, vmem],
        out_specs=(vmem, vmem),
        out_shape=(
            jax.ShapeDtypeStruct((CZ, rows, cols), f32),
            jax.ShapeDtypeStruct((1, CZ, rows, cols), f32),
        ),
        scratch_shapes=[
            pltpu.VMEM((slabs, tall, cols), f32),
            pltpu.VMEM((views, tap_rows, cols), f32),
            pltpu.VMEM((views, 3 * CZ, wide, cols), f32),
            pltpu.VMEM((3 * CZ, wide, cols), f32),
            pltpu.VMEM((3 * CZ, wide, cols), f32),
            pltpu.VMEM((views, 2, 2 * cols, 2 * cols), jnp.bfloat16),
            pltpu.VMEM((CZ + 2 * margin, wide, cols), f32),
            pltpu.VMEM((CZ + 2 * margin, strip + 2 * margin, cols), f32),
            pltpu.VMEM((CZ + 2 * margin, strip + 2 * margin, cols), f32),
            pltpu.VMEM((CZ, strip, cols), f32),
            pltpu.VMEM((CZ, strip, cols), f32),
            dma((slabs,)), dma((slabs,)), dma, dma((views,)), dma((views,)),
            dma((views,)), dma((views,)), dma, dma((views,)), dma, dma((views,)), dma((2,)),
            dma((2, views)), dma((2, views)), dma((8,)), dma((8,)), dma((views,)), dma((views,)),
        ],
        compiler_params=pltpu.CompilerParams(
            collective_id=0, has_side_effects=True, vmem_limit_bytes=40 * 1024 * 1024),
        name="world",
    )(shift_frac[0], acc, tap_rows_all)
    return estimate, joined


def solution(mesh):
    dims = (mesh.shape["gz"], mesh.shape["view"], mesh.shape["gy"])
    return jax.shard_map(
        functools.partial(on_device, dims),
        mesh=mesh,
        in_specs=(
            P("view", ("groups", "gz"), None, "gy", None),
            P("view", "gy", ("groups", "gz")),
            P("view", "gy", ("groups", "gz"), None),
            P("view", "gy", ("groups", "gz")),
            P("view", None),
            P("view", None, None),
        ),
        out_specs=(P(("groups", "gz"), "gy", None), P("view", ("groups", "gz"), "gy", None)),
        check_vma=False,
    )
```
